32 devices in a mesh: groups: 2 (over x), width: 16 (over z, y, core).
Axes of the slice: x: 2, y: 2, z: 4, core: 2. Of those that a mesh axis runs over, the one named last changes fastest.
Arguments:
- stream_in: bfloat16 [2, 128, 8192], P(None, 'groups', 'width'), parts along dimension 1, may hold values from -16 to 16
- norm_gain: float32 [2, 8192], replicated, may hold values from 0.1 to 1.9
- w_gate: bfloat16 [2, 8192, 14336], P(None, None, 'width'), may hold values from -0.0625 to 0.0625
- w_up: bfloat16 [2, 8192, 14336], P(None, None, 'width'), may hold values from -0.0625 to 0.0625
- w_down: bfloat16 [2, 14336, 8192], P(None, 'width'), may hold values from -0.0625 to 0.0625
Outputs:
- stream_out: bfloat16 [2, 128, 8192], P(None, 'groups', 'width'), parts along dimension 1
The draws below stay inside these ranges and needn't reach their ends.
There are 2 independent parts, one for each index of `groups`. The reference program is written for one: setup_inputs(seed, part) draws one part's arguments, and reference() takes and returns one part's arrays. A program takes and returns all parts, laid end to end along the dimension named above; an argument that names none is the same for every part. Nothing has to cross between parts.
All inputs are finite; a program needn't handle non-finite values.
Results may differ from the reference program's by a relative error of at most 0.012.
Values may be sent and summed in bfloat16 or wider, within the bound.
A program may use at most 192 MiB of HBM per device.

```python
import math
import jax
import jax.numpy as jnp
from jax import lax

D = 8192
FF = 14336
LAYERS = 2
MICRO = 2
ROWS = 64


def draw_stream_in(key, part):
    key_base, key_column, key_row = jax.random.split(key, 3)
    column_pos = jnp.arange(D, dtype=jnp.float32) / (D - 1)
    column_scale = 3.0 ** column_pos / 3.0 * jnp.exp(jax.random.uniform(key_column, (D,), jnp.float32, math.log(0.55), math.log(1.8)))
    base_values = jax.random.normal(key_base, (MICRO, ROWS, D), jnp.float32)
    row_scale = jnp.exp(jax.random.uniform(key_row, (MICRO, ROWS, 1), jnp.float32, math.log(0.3), math.log(3.0)))
    values = jnp.clip(base_values * row_scale * column_scale, -16.0, 16.0)
    return values.astype(jnp.bfloat16)


def with_spikes(array, key, source, target, parts, factor):
    owner, partner = [(jnp.arange(array.shape[dim]) // (array.shape[dim] // parts)).reshape([-1 if axis == dim else 1 for axis in range(array.ndim)]) for dim in (source, target)]
    chosen = jax.random.permutation(key, parts)[partner]
    strong = (owner == chosen) | (owner == (partner + parts // 2) % parts)
    return jnp.where(strong, factor * array, array)


def level_of(stream_key, extent, shards, smallest, top_value):
    def one(position, blocks):
        draws = jax.random.uniform(jax.random.fold_in(jax.random.fold_in(stream_key, 6), position), (blocks,), jnp.float32, smallest / len(shards), top_value / len(shards))
        return jnp.repeat(jnp.exp(draws), extent[position] // blocks).reshape((-1,) + (1,) * (len(extent) - position - 1))

    factor_of = one(*shards[0])
    for cut in shards[1:]:
        factor_of = factor_of * one(*cut)
    return factor_of


def bell_draw(key, extent, width, limit, cuts=(), kind=jnp.bfloat16):
    drawn = width * jax.random.normal(key, extent, jnp.float32)
    if cuts:
        drawn = drawn * level_of(key, extent, cuts, -0.22, 0.18)
    return jnp.clip(drawn, -limit, limit).astype(kind)


def bell_draw_with(key, shape, deviation, limit, pieces, heavy, kind=jnp.bfloat16):
    values = deviation * jax.random.normal(key, shape, jnp.float32)
    if pieces:
        values = values * level_of(key, shape, pieces, -0.22, 0.18)
    return jnp.clip(with_spikes(values, jax.random.fold_in(key, 3), *heavy), -limit, limit).astype(kind)


def setup_inputs(seed: int = 0, part: int = 0) -> dict:
    seeds = jax.random.split(jax.random.key(seed), 6)
    own_keys = jax.random.split(jax.random.fold_in(seeds[5], part), 6)
    stream_in = draw_stream_in(jax.random.fold_in(jax.random.fold_in(seeds[5], part), 71), part)
    norm_gain = jnp.clip(1.0 + 0.18 * jax.random.normal(seeds[1], (LAYERS, D), jnp.float32), 0.1, 1.9)
    w_gate = bell_draw(seeds[2], (LAYERS, D, FF), D ** -0.5, 0.0625, ((2, 16),))
    w_up = bell_draw(seeds[3], (LAYERS, D, FF), D ** -0.5, 0.0625, ((2, 16),))
    w_down = bell_draw_with(seeds[4], (LAYERS, FF, D), FF ** -0.5, 0.0625, ((1, 16),), (1, 2, 16, 2.0))
    return dict(stream_in=stream_in, norm_gain=norm_gain, w_gate=w_gate, w_up=w_up, w_down=w_down)


def sublayer(stream, gain_row, gate_weight, up_weight, down_weight):
    stream_f = stream.astype(jnp.float32)
    meansq = lax.optimization_barrier(jnp.mean(stream_f * stream_f, axis=1, keepdims=True))
    normed = (stream_f * lax.rsqrt(meansq + 1e-05) * gain_row).astype(jnp.bfloat16)
    gate_out = jnp.dot(normed, gate_weight, preferred_element_type=jnp.float32)
    up_out = jnp.dot(normed, up_weight, preferred_element_type=jnp.float32)
    hidden = (jax.nn.silu(gate_out) * up_out).astype(jnp.bfloat16)
    branch = jnp.dot(hidden, down_weight, preferred_element_type=jnp.float32)
    return (stream_f + branch).astype(jnp.bfloat16)

def reference(stream_in, norm_gain, w_gate, w_up, w_down):
    results = []
    for micro_index in range(MICRO):
        stream = stream_in[micro_index]
        for depth in range(LAYERS):
            stream = sublayer(stream, norm_gain[depth], w_gate[depth], w_up[depth], w_down[depth])
        results.append(stream)
    return jnp.stack(results)
```

```python
import functools

import jax
import jax.numpy as jnp
from jax import lax
from jax.experimental import pallas as pl
from jax.experimental.pallas import tpu as pltpu
from jax.sharding import PartitionSpec as P

MESH = pl.DeviceIdType.MESH


def plain_body(stream_in, norm_gain, w_gate, w_up, w_down):
    micro, rows, own_width = stream_in.shape
    stream = stream_in.reshape(micro * rows, own_width)
    for depth in range(w_gate.shape[0]):
        whole = lax.all_gather(stream, "width", axis=1, tiled=True).astype(jnp.float32)
        meansq = jnp.mean(whole * whole, axis=1, keepdims=True)
        normed = (whole * lax.rsqrt(meansq + 1e-05) * norm_gain[depth]).astype(jnp.bfloat16)
        gate_out = jnp.dot(normed, w_gate[depth], preferred_element_type=jnp.float32)
        up_out = jnp.dot(normed, w_up[depth], preferred_element_type=jnp.float32)
        hidden = (jax.nn.silu(gate_out) * up_out).astype(jnp.bfloat16)
        partials = jnp.dot(hidden, w_down[depth], preferred_element_type=jnp.float32)
        branch = lax.psum_scatter(partials, "width", scatter_dimension=1, tiled=True)
        stream = (stream.astype(jnp.float32) + branch).astype(jnp.bfloat16)
    return stream.reshape(micro, rows, own_width)


def solution(mesh):
    return jax.shard_map(
        plain_body,
        mesh=mesh,
        in_specs=(
            P(None, "groups", "width"),
            P(),
            P(None, None, "width"),
            P(None, None, "width"),
            P(None, "width", None),
        ),
        out_specs=P(None, "groups", "width"),
        check_vma=False,
    )
```

```python
import functools

import jax
import jax.numpy as jnp
from jax import lax
from jax.experimental import pallas as pl
from jax.experimental.pallas import tpu as pltpu
from jax.sharding import PartitionSpec as P

MESH = pl.DeviceIdType.MESH


def plain_body(stream_in, norm_gain, w_gate, w_up, w_down):
    micro, rows, own_width = stream_in.shape
    stream = stream_in.reshape(micro * rows, own_width)
    for depth in range(w_gate.shape[0]):
        whole = lax.all_gather(stream, "width", axis=1, tiled=True).astype(jnp.float32)
        meansq = jnp.mean(whole * whole, axis=1, keepdims=True)
        normed = (whole * lax.rsqrt(meansq + 1e-05) * norm_gain[depth]).astype(jnp.bfloat16)
        gate_out = jnp.dot(normed, w_gate[depth], preferred_element_type=jnp.float32)
        up_out = jnp.dot(normed, w_up[depth], preferred_element_type=jnp.float32)
        hidden = (jax.nn.silu(gate_out) * up_out).astype(jnp.bfloat16)
        partials = jnp.dot(hidden, w_down[depth], preferred_element_type=jnp.float32)
        branch = lax.psum_scatter(partials, "width", scatter_dimension=1, tiled=True)
        stream = (stream.astype(jnp.float32) + branch).astype(jnp.bfloat16)
    return stream.reshape(micro, rows, own_width)


def kernel(
    n, x_ref, gain_ref, wg_ref, wu_ref, wd_ref, out_ref,
    pair_w, down_w, parts, scaled, acc, squares, hidden, own,
    core_out, core_in, y_out, y_in, z_out, z_in, keep,
    pair_sem, down_sem, gather_send, gather_recv, sum_send, core_recv, y_recv, z_recv,
):
    layers = wg_ref.shape[0]
    chips, nz = n // 2, n // 4
    width = x_ref.shape[1]
    chunk = 2 * width
    me = lax.axis_index("width")
    c, y, z = lax.rem(me, 2), lax.rem(me // 2, 2), me // 4

    def device(zi, yi, ci):
        return (zi * 2 + yi) * 2 + ci

    core_peer, y_peer = device(z, y, 1 - c), device(z, 1 - y, c)

    def turn(step):
        return lax.rem(z + step, nz)

    def pair_copy(depth, chip, j):
        src = wg_ref if j == 0 else wu_ref
        rows = pl.ds(pl.multiple_of(chip * chunk, chunk), chunk)
        return pltpu.make_async_copy(src.at[depth, rows, :], pair_w.at[chip, j], pair_sem.at[chip, j])

    def down_copy(depth, dev):
        cols = pl.ds(pl.multiple_of(dev * width, width), width)
        return pltpu.make_async_copy(wd_ref.at[depth, :, cols], down_w.at[dev], down_sem.at[dev])

    def remote(src, dst, send, recv, dev):
        return pltpu.make_async_remote_copy(
            src_ref=src, dst_ref=dst, send_sem=send, recv_sem=recv,
            device_id={"width": dev}, device_id_type=MESH,
        )

    def load_pairs(chip):
        pair_copy(0, chip, 0).start()
        pair_copy(0, chip, 1).start()

    load_pairs(z * 2 + y)

    barrier = pltpu.get_barrier_semaphore()
    peers = [core_peer, y_peer] + [device(turn(j), y, c) for j in range(1, nz)]
    for peer in peers:
        pl.semaphore_signal(barrier, inc=1, device_id={"width": peer}, device_id_type=MESH)

    for k in range(1, nz):
        load_pairs(turn(k) * 2 + y)
        load_pairs(turn(k - 1) * 2 + 1 - y)
    load_pairs(turn(nz - 1) * 2 + 1 - y)

    def down_chip(t):
        return turn(lax.rem(t, nz) + 1) * 2 + jnp.where(t < nz, 1 - y, y)

    @pl.loop(0, chips)
    def _(t):
        chip = down_chip(t)
        down_copy(0, chip * 2 + 1 - c).start()
        down_copy(0, chip * 2 + c).start()

    pl.semaphore_wait(barrier, len(peers))

    for depth in range(layers):
        mine = x_ref if depth == 0 else own.at[depth]

        def to_peer(src, owner, slot, dev):
            return remote(src, parts.at[depth, owner], gather_send.at[depth, slot], gather_recv.at[depth, owner], dev)

        def arrived(owner):
            to_peer(mine, owner, 0, core_peer).wait_recv()

        to_peer(mine, me, nz - 1, y_peer).start()
        for j in range(1, nz):
            to_peer(mine, me, j - 1, device(turn(nz - j), y, c)).start()
        to_peer(mine, me, 2 * nz - 1, core_peer).start()
        parts[depth, me] = mine[...]
        acc[...] = jnp.zeros_like(acc)
        squares[...] = jnp.zeros_like(squares)

        def gate_up(chip):
            for h in range(2):
                piece = parts[depth, chip * 2 + h].astype(jnp.float32)
                cols = pl.ds(pl.multiple_of((chip * 2 + h) * width, width), width)
                scaled[:, h * width:(h + 1) * width] = (piece * gain_ref[depth:depth + 1, cols]).astype(jnp.bfloat16)
                sq = piece * piece
                total = sq[:, :128]
                for i in range(1, width // 128):
                    total = total + sq[:, i * 128:(i + 1) * 128]
                squares[...] += total
            for j in range(2):
                pair_copy(depth, chip, j).wait()

            @pl.loop(0, 2)
            def _(j):
                acc[j] += jnp.dot(scaled[...], pair_w[chip, j], preferred_element_type=jnp.float32)

            if depth + 1 < layers:
                for j in range(2):
                    pair_copy(depth + 1, chip, j).start()

        @pl.loop(0, nz + 1)
        def _(k):
            @pl.when(k < nz)
            def _():
                chip = turn(k) * 2 + y
                arrived(chip * 2 + 1 - c)
                gate_up(chip)

            @pl.when(k + 1 < nz)
            def _():
                owner = device(turn(k + 1), y, c)
                arrived(owner)
                to_peer(parts.at[depth, owner], owner, nz + k, y_peer).start()
                to_peer(parts.at[depth, owner], owner, 2 * nz + k, core_peer).start()

            @pl.when(k < nz)
            def _():
                owner = device(turn(k), 1 - y, c)
                arrived(owner)
                to_peer(parts.at[depth, owner], owner, 3 * nz - 1 + k, core_peer).start()

            @pl.when(k > 0)
            def _():
                chip = turn(k - 1) * 2 + 1 - y
                arrived(chip * 2 + 1 - c)
                gate_up(chip)

        meansq = jnp.sum(squares[...], axis=1, keepdims=True) / (n * width)
        scale = lax.rsqrt(meansq + 1e-05)
        gate_out = acc[0] * scale
        hidden[...] = (gate_out / (1.0 + jnp.exp(-gate_out)) * (acc[1] * scale)).astype(jnp.bfloat16)

        def core_copy(chip):
            return remote(core_out.at[depth, chip], core_in.at[depth, chip],
                          sum_send.at[depth, chip], core_recv.at[depth, chip], core_peer)

        def y_copy(zi):
            return remote(y_out.at[depth, zi], y_in.at[depth, zi],
                          sum_send.at[depth, chips + zi], y_recv.at[depth, zi], y_peer)

        def z_copy(zi, slot):
            return remote(z_out.at[depth, zi], z_in.at[depth, slot],
                          sum_send.at[depth, chips + nz + zi], z_recv.at[depth, slot], device(zi, y, c))

        def down(dev):
            down_copy(depth, dev).wait()
            return jnp.dot(hidden[...], down_w[dev], preferred_element_type=jnp.float32)

        @pl.loop(0, chips)
        def _(t):
            chip = down_chip(t)
            core_out[depth, chip] = down(chip * 2 + 1 - c).astype(jnp.bfloat16)
            core_copy(chip).start()
            keep[chip] = down(chip * 2 + c)
            if depth + 1 < layers:
                down_copy(depth + 1, chip * 2 + 1 - c).start()
                down_copy(depth + 1, chip * 2 + c).start()

            @pl.when((t > 0) & (t <= nz))
            def _():
                zi = turn(t)
                far = zi * 2 + 1 - y
                core_copy(far).wait_recv()
                y_out[depth, zi] = (keep[far] + core_in[depth, far].astype(jnp.float32)).astype(jnp.bfloat16)
                y_copy(zi).start()

        def near(zi):
            chip = zi * 2 + y
            core_copy(chip).wait_recv()
            total = keep[chip] + core_in[depth, chip].astype(jnp.float32)
            y_copy(zi).wait_recv()
            return total + y_in[depth, zi].astype(jnp.float32)

        @pl.loop(1, nz)
        def _(k):
            zi = turn(k)
            z_out[depth, zi] = near(zi).astype(jnp.bfloat16)
            z_copy(zi, z).start()

        total = near(z) + mine[...].astype(jnp.float32)
        for k in range(1, nz):
            zi = turn(k)
            z_copy(zi, zi).wait_recv()
            total = total + z_in[depth, zi].astype(jnp.float32)
        if depth + 1 < layers:
            own[depth + 1] = total.astype(jnp.bfloat16)
        else:
            out_ref[...] = total.astype(jnp.bfloat16)

    for depth in range(layers):
        @pl.loop(0, n - 1)
        def _(i):
            remote(x_ref, parts.at[depth, me], gather_send.at[depth, i], gather_recv.at[depth, me], core_peer).wait_send()

        @pl.loop(0, chips + nz)
        def _(i):
            remote(x_ref, parts.at[depth, me], sum_send.at[depth, i], gather_recv.at[depth, me], core_peer).wait_send()

        for k in range(1, nz):
            remote(x_ref, parts.at[depth, me], sum_send.at[depth, chips + nz + turn(k)], gather_recv.at[depth, me], core_peer).wait_send()


def fused(n, stream_in, norm_gain, w_gate, w_up, w_down):
    micro, rows, width = stream_in.shape
    layers, d, ff = w_gate.shape
    m, chips, nz = micro * rows, n // 2, n // 4
    bf, f32, dma = jnp.bfloat16, jnp.float32, pltpu.SemaphoreType.DMA
    vmem = pl.BlockSpec(memory_space=pltpu.VMEM)
    hbm = pl.BlockSpec(memory_space=pltpu.HBM)
    out = pl.pallas_call(
        functools.partial(kernel, n),
        out_shape=jax.ShapeDtypeStruct((m, width), bf),
        in_specs=[vmem, vmem, hbm, hbm, hbm],
        out_specs=vmem,
        scratch_shapes=[
            pltpu.VMEM((chips, 2, 2 * width, ff), bf),
            pltpu.VMEM((n, ff, width), bf),
            pltpu.VMEM((layers, n, m, width), bf),
            pltpu.VMEM((m, 2 * width), bf),
            pltpu.VMEM((2, m, ff), f32),
            pltpu.VMEM((m, 128), f32),
            pltpu.VMEM((m, ff), bf),
            pltpu.VMEM((layers, m, width), bf),
            pltpu.VMEM((layers, chips, m, width), bf),
            pltpu.VMEM((layers, chips, m, width), bf),
            pltpu.VMEM((layers, nz, m, width), bf),
            pltpu.VMEM((layers, nz, m, width), bf),
            pltpu.VMEM((layers, nz, m, width), bf),
            pltpu.VMEM((layers, nz, m, width), bf),
            pltpu.VMEM((chips, m, width), f32),
            dma((chips, 2)),
            dma((n,)),
            dma((layers, n - 1)),
            dma((layers, n)),
            dma((layers, chips + 2 * nz)),
            dma((layers, chips)),
            dma((layers, nz)),
            dma((layers, nz)),
        ],
        compiler_params=pltpu.CompilerParams(
            collective_id=0, has_side_effects=True, vmem_limit_bytes=67_043_328
        ),
    )(stream_in.reshape(m, width), norm_gain, w_gate, w_up, w_down)
    return out.reshape(micro, rows, width)


def body(n, stream_in, norm_gain, w_gate, w_up, w_down):
    aligned = stream_in.shape[2] % 128 == 0 and w_gate.shape[2] % 128 == 0 and n % 4 == 0
    held = w_gate[0].size * 6
    if aligned and n > 4 and held < 48 * 2**20:
        return fused(n, stream_in, norm_gain, w_gate, w_up, w_down)
    return plain_body(stream_in, norm_gain, w_gate, w_up, w_down)


def solution(mesh):
    return jax.shard_map(
        functools.partial(body, mesh.shape["width"]),
        mesh=mesh,
        in_specs=(
            P(None, "groups", "width"),
            P(),
            P(None, None, "width"),
            P(None, None, "width"),
            P(None, "width", None),
        ),
        out_specs=P(None, "groups", "width"),
        check_vma=False,
    )
```

```python
import functools

import jax
import jax.numpy as jnp
from jax import lax
from jax.experimental import pallas as pl
from jax.experimental.pallas import tpu as pltpu
from jax.sharding import PartitionSpec as P

MESH = pl.DeviceIdType.MESH


def plain_body(stream_in, norm_gain, w_gate, w_up, w_down):
    micro, rows, own_width = stream_in.shape
    stream = stream_in.reshape(micro * rows, own_width)
    for depth in range(w_gate.shape[0]):
        whole = lax.all_gather(stream, "width", axis=1, tiled=True).astype(jnp.float32)
        meansq = jnp.mean(whole * whole, axis=1, keepdims=True)
        normed = (whole * lax.rsqrt(meansq + 1e-05) * norm_gain[depth]).astype(jnp.bfloat16)
        gate_out = jnp.dot(normed, w_gate[depth], preferred_element_type=jnp.float32)
        up_out = jnp.dot(normed, w_up[depth], preferred_element_type=jnp.float32)
        hidden = (jax.nn.silu(gate_out) * up_out).astype(jnp.bfloat16)
        partials = jnp.dot(hidden, w_down[depth], preferred_element_type=jnp.float32)
        branch = lax.psum_scatter(partials, "width", scatter_dimension=1, tiled=True)
        stream = (stream.astype(jnp.float32) + branch).astype(jnp.bfloat16)
    return stream.reshape(micro, rows, own_width)


def kernel(
    n, x_ref, gain_ref, wg_ref, wu_ref, wd_ref, out_ref,
    pair_w, down_w, parts, scaled, acc, squares, hidden, own,
    core_out, core_in, y_out, y_in, z_out, z_in, keep,
    pair_sem, down_sem, gather_send, gather_recv, sum_send, core_recv, y_recv, z_recv,
):
    layers = wg_ref.shape[0]
    chips, nz = n // 2, n // 4
    width = x_ref.shape[1]
    chunk = 2 * width
    me = lax.axis_index("width")
    c, y, z = lax.rem(me, 2), lax.rem(me // 2, 2), me // 4

    def device(zi, yi, ci):
        return (zi * 2 + yi) * 2 + ci

    core_peer, y_peer = device(z, y, 1 - c), device(z, 1 - y, c)

    def turn(step):
        return lax.rem(z + step, nz)

    low = z < nz // 2

    def order(k):
        rank = k - 1 + jnp.where(k - 1 >= jnp.where(low, z, nz - 1 - z), 1, 0)
        return jnp.where(k == 0, z, jnp.where(low, rank, nz - 1 - rank))

    def pair_copy(depth, chip, j):
        src = wg_ref if j == 0 else wu_ref
        rows = pl.ds(pl.multiple_of(chip * chunk, chunk), chunk)
        return pltpu.make_async_copy(src.at[depth, rows, :], pair_w.at[chip, j], pair_sem.at[chip, j])

    def down_copy(depth, dev):
        cols = pl.ds(pl.multiple_of(dev * width, width), width)
        return pltpu.make_async_copy(wd_ref.at[depth, :, cols], down_w.at[dev], down_sem.at[dev])

    def remote(src, dst, send, recv, dev):
        return pltpu.make_async_remote_copy(
            src_ref=src, dst_ref=dst, send_sem=send, recv_sem=recv,
            device_id={"width": dev}, device_id_type=MESH,
        )

    def load_pairs(chip):
        pair_copy(0, chip, 0).start()
        pair_copy(0, chip, 1).start()

    load_pairs(z * 2 + y)

    barrier = pltpu.get_barrier_semaphore()
    peers = [core_peer, y_peer] + [device(turn(j), y, c) for j in range(1, nz)]
    for peer in peers:
        pl.semaphore_signal(barrier, inc=1, device_id={"width": peer}, device_id_type=MESH)

    for k in range(1, nz):
        load_pairs(order(k) * 2 + y)
        load_pairs(order(k - 1) * 2 + 1 - y)
    load_pairs(order(nz - 1) * 2 + 1 - y)

    def down_chip(t):
        return turn(lax.rem(t, nz) + 1) * 2 + jnp.where(t < nz, 1 - y, y)

    @pl.loop(0, chips)
    def _(t):
        chip = down_chip(t)
        down_copy(0, chip * 2 + 1 - c).start()
        down_copy(0, chip * 2 + c).start()

    pl.semaphore_wait(barrier, len(peers))

    for depth in range(layers):
        mine = x_ref if depth == 0 else own.at[depth]

        def to_peer(src, owner, slot, dev):
            return remote(src, parts.at[depth, owner], gather_send.at[depth, slot], gather_recv.at[depth, owner], dev)

        def arrived(owner):
            to_peer(mine, owner, 0, core_peer).wait_recv()

        to_peer(mine, me, nz - 1, y_peer).start()

        @pl.when(z < nz - 1)
        def _():
            to_peer(mine, me, n - 1 + z, device(z + 1, y, c)).start()

        @pl.when(z > 0)
        def _():
            to_peer(mine, me, n - 1 + nz, device(z - 1, y, c)).start()

        to_peer(mine, me, 2 * nz - 1, core_peer).start()
        parts[depth, me] = mine[...]
        acc[...] = jnp.zeros_like(acc)
        squares[...] = jnp.zeros_like(squares)

        def gate_up(chip):
            for h in range(2):
                piece = parts[depth, chip * 2 + h].astype(jnp.float32)
                cols = pl.ds(pl.multiple_of((chip * 2 + h) * width, width), width)
                scaled[:, h * width:(h + 1) * width] = (piece * gain_ref[depth:depth + 1, cols]).astype(jnp.bfloat16)
                sq = piece * piece
                total = sq[:, :128]
                for i in range(1, width // 128):
                    total = total + sq[:, i * 128:(i + 1) * 128]
                squares[...] += total
            for j in range(2):
                pair_copy(depth, chip, j).wait()

            @pl.loop(0, 2)
            def _(j):
                acc[j] += jnp.dot(scaled[...], pair_w[chip, j], preferred_element_type=jnp.float32)

            if depth + 1 < layers:
                for j in range(2):
                    pair_copy(depth + 1, chip, j).start()

        @pl.loop(0, nz + 1)
        def _(k):
            @pl.when(k < nz)
            def _():
                chip = order(k) * 2 + y
                arrived(chip * 2 + 1 - c)
                gate_up(chip)

            @pl.when(k + 1 < nz)
            def _():
                zi = order(k + 1)
                owner = device(zi, y, c)
                arrived(owner)

                @pl.when((zi < z) & (z < nz - 1))
                def _():
                    to_peer(parts.at[depth, owner], owner, n - 1 + zi, device(z + 1, y, c)).start()

                @pl.when((zi > z) & (z > 0))
                def _():
                    to_peer(parts.at[depth, owner], owner, n - 1 + zi, device(z - 1, y, c)).start()

                to_peer(parts.at[depth, owner], owner, nz + k, y_peer).start()
                to_peer(parts.at[depth, owner], owner, 2 * nz + k, core_peer).start()

            @pl.when(k < nz)
            def _():
                owner = device(order(k), 1 - y, c)
                arrived(owner)
                to_peer(parts.at[depth, owner], owner, 3 * nz - 1 + k, core_peer).start()

            @pl.when(k > 0)
            def _():
                chip = order(k - 1) * 2 + 1 - y
                arrived(chip * 2 + 1 - c)
                gate_up(chip)

        meansq = jnp.sum(squares[...], axis=1, keepdims=True) / (n * width)
        scale = lax.rsqrt(meansq + 1e-05)
        gate_out = acc[0] * scale
        hidden[...] = (gate_out / (1.0 + jnp.exp(-gate_out)) * (acc[1] * scale)).astype(jnp.bfloat16)

        def core_copy(chip):
            return remote(core_out.at[depth, chip], core_in.at[depth, chip],
                          sum_send.at[depth, chip], core_recv.at[depth, chip], core_peer)

        def y_copy(zi):
            return remote(y_out.at[depth, zi], y_in.at[depth, zi],
                          sum_send.at[depth, chips + zi], y_recv.at[depth, zi], y_peer)

        def z_copy(zi, slot):
            return remote(z_out.at[depth, zi], z_in.at[depth, slot],
                          sum_send.at[depth, chips + nz + zi], z_recv.at[depth, slot], device(zi, y, c))

        def down(dev):
            down_copy(depth, dev).wait()
            return jnp.dot(hidden[...], down_w[dev], preferred_element_type=jnp.float32)

        @pl.loop(0, chips)
        def _(t):
            chip = down_chip(t)
            core_out[depth, chip] = down(chip * 2 + 1 - c).astype(jnp.bfloat16)
            core_copy(chip).start()
            keep[chip] = down(chip * 2 + c)
            if depth + 1 < layers:
                down_copy(depth + 1, chip * 2 + 1 - c).start()
                down_copy(depth + 1, chip * 2 + c).start()

            @pl.when((t > 0) & (t <= nz))
            def _():
                zi = turn(t)
                far = zi * 2 + 1 - y
                core_copy(far).wait_recv()
                y_out[depth, zi] = (keep[far] + core_in[depth, far].astype(jnp.float32)).astype(jnp.bfloat16)
                y_copy(zi).start()

        def near(zi):
            chip = zi * 2 + y
            core_copy(chip).wait_recv()
            total = keep[chip] + core_in[depth, chip].astype(jnp.float32)
            y_copy(zi).wait_recv()
            return total + y_in[depth, zi].astype(jnp.float32)

        @pl.loop(1, nz)
        def _(k):
            zi = turn(k)
            z_out[depth, zi] = near(zi).astype(jnp.bfloat16)
            z_copy(zi, z).start()

        total = near(z) + mine[...].astype(jnp.float32)
        for k in range(1, nz):
            zi = turn(k)
            z_copy(zi, zi).wait_recv()
            total = total + z_in[depth, zi].astype(jnp.float32)
        if depth + 1 < layers:
            own[depth + 1] = total.astype(jnp.bfloat16)
        else:
            out_ref[...] = total.astype(jnp.bfloat16)

    for depth in range(layers):
        def gather_sent(i):
            remote(x_ref, parts.at[depth, me], gather_send.at[depth, i], gather_recv.at[depth, me], core_peer).wait_send()

        @pl.loop(0, nz)
        def _(zi):
            @pl.when(((zi <= z) & (z < nz - 1)) | ((zi > z) & (z > 0)))
            def _():
                gather_sent(n - 1 + zi)

        @pl.when(z > 0)
        def _():
            gather_sent(n - 1 + nz)

        @pl.loop(nz - 1, n - 1)
        def _(i):
            remote(x_ref, parts.at[depth, me], gather_send.at[depth, i], gather_recv.at[depth, me], core_peer).wait_send()

        @pl.loop(0, chips + nz)
        def _(i):
            remote(x_ref, parts.at[depth, me], sum_send.at[depth, i], gather_recv.at[depth, me], core_peer).wait_send()

        for k in range(1, nz):
            remote(x_ref, parts.at[depth, me], sum_send.at[depth, chips + nz + turn(k)], gather_recv.at[depth, me], core_peer).wait_send()


def fused(n, stream_in, norm_gain, w_gate, w_up, w_down):
    micro, rows, width = stream_in.shape
    layers, d, ff = w_gate.shape
    m, chips, nz = micro * rows, n // 2, n // 4
    bf, f32, dma = jnp.bfloat16, jnp.float32, pltpu.SemaphoreType.DMA
    vmem = pl.BlockSpec(memory_space=pltpu.VMEM)
    hbm = pl.BlockSpec(memory_space=pltpu.HBM)
    out = pl.pallas_call(
        functools.partial(kernel, n),
        out_shape=jax.ShapeDtypeStruct((m, width), bf),
        in_specs=[vmem, vmem, hbm, hbm, hbm],
        out_specs=vmem,
        scratch_shapes=[
            pltpu.VMEM((chips, 2, 2 * width, ff), bf),
            pltpu.VMEM((n, ff, width), bf),
            pltpu.VMEM((layers, n, m, width), bf),
            pltpu.VMEM((m, 2 * width), bf),
            pltpu.VMEM((2, m, ff), f32),
            pltpu.VMEM((m, 128), f32),
            pltpu.VMEM((m, ff), bf),
            pltpu.VMEM((layers, m, width), bf),
            pltpu.VMEM((layers, chips, m, width), bf),
            pltpu.VMEM((layers, chips, m, width), bf),
            pltpu.VMEM((layers, nz, m, width), bf),
            pltpu.VMEM((layers, nz, m, width), bf),
            pltpu.VMEM((layers, nz, m, width), bf),
            pltpu.VMEM((layers, nz, m, width), bf),
            pltpu.VMEM((chips, m, width), f32),
            dma((chips, 2)),
            dma((n,)),
            dma((layers, n + nz)),
            dma((layers, n)),
            dma((layers, chips + 2 * nz)),
            dma((layers, chips)),
            dma((layers, nz)),
            dma((layers, nz)),
        ],
        compiler_params=pltpu.CompilerParams(
            collective_id=0, has_side_effects=True, vmem_limit_bytes=67_043_328
        ),
    )(stream_in.reshape(m, width), norm_gain, w_gate, w_up, w_down)
    return out.reshape(micro, rows, width)


def body(n, stream_in, norm_gain, w_gate, w_up, w_down):
    aligned = stream_in.shape[2] % 128 == 0 and w_gate.shape[2] % 128 == 0 and n % 4 == 0
    held = w_gate[0].size * 6
    if aligned and n > 4 and held < 48 * 2**20:
        return fused(n, stream_in, norm_gain, w_gate, w_up, w_down)
    return plain_body(stream_in, norm_gain, w_gate, w_up, w_down)


def solution(mesh):
    return jax.shard_map(
        functools.partial(body, mesh.shape["width"]),
        mesh=mesh,
        in_specs=(
            P(None, "groups", "width"),
            P(),
            P(None, None, "width"),
            P(None, None, "width"),
            P(None, "width", None),
        ),
        out_specs=P(None, "groups", "width"),
        check_vma=False,
    )
```
